32 devices in a mesh: noise: 8 (over z, x), qi: 2 (over core), kj: 2 (over y).
Axes of the slice: x: 2, y: 2, z: 4, core: 2. Of those that a mesh axis runs over, the one named last changes fastest.
Arguments:
- pair_rep: bfloat16 [128, 2, 64, 128], P('qi', None, 'kj'), may hold values from -6 to 6
- query_rows: bfloat16 [8, 128, 768], P('noise', 'qi'), may hold values from -10 to 10
- key_rows: bfloat16 [8, 2, 64, 768], P('noise', None, 'kj'), may hold values from -10 to 10
- value_rows: bfloat16 [8, 2, 64, 768], P('noise', None, 'kj'), may hold values from -6 to 6
- output_grad: bfloat16 [8, 128, 768], P('noise', 'qi'), may hold values from -24 to 24
- gain_first: float32 [128], replicated, may hold values from 0.5 to 1.5
- gate_weight: bfloat16 [128, 512], replicated, may hold values from -0.5 to 0.5
- up_weight: bfloat16 [128, 512], replicated, may hold values from -0.5 to 0.5
- down_weight: bfloat16 [512, 128], replicated, may hold values from -0.25 to 0.25
- gain_second: float32 [128], replicated, may hold values from 0.5 to 1.5
- head_weight: bfloat16 [128, 16], replicated, may hold values from -0.5 to 0.5
Outputs:
- query_grad: bfloat16 [8, 128, 768], P('noise', ('qi', 'kj'))
- key_grad: bfloat16 [8, 128, 768], P('noise', ('qi', 'kj'))
- value_grad: bfloat16 [8, 128, 768], P('noise', ('qi', 'kj'))
- pair_grad: bfloat16 [2, 8, 8, 2, 64, 128], P('qi', 'noise', None, None, 'kj')
- gate_grad: float32 [128, 512], replicated
- up_grad: float32 [128, 512], replicated
- down_grad: float32 [512, 128], replicated
- head_grad: float32 [128, 16], replicated
- first_grad: float32 [128], replicated
- second_grad: float32 [128], replicated
The draws below stay inside these ranges and needn't reach their ends.
All inputs are finite; a program needn't handle non-finite values.
Results may differ from the reference program's by a relative error of at most 0.011.
Values may be sent and summed in bfloat16 or wider, within the bound.
A program may use at most 64 MiB of HBM per device.

```python
import jax
import jax.numpy as jnp
from jax import lax

HEADS = 16
HEAD_DIM = 48
PAIR = 128
FF = 512
WIDTH = 768
TOKENS = 128
QUERY_TILE = 64
ROWS_SUB = 8
COPIES = 8
N_QI = 2


def drawn_draw(key):
    base_key = jax.random.fold_in(key, 4242)
    first_key, second_key = jax.random.split(base_key, 2)
    full_shape = (COPIES, TOKENS, HEADS, HEAD_DIM)
    queries = jnp.clip(jax.random.normal(first_key, full_shape, jnp.float32), -6.0, 6.0)
    keyset = jnp.clip(jax.random.normal(second_key, full_shape, jnp.float32), -6.0, 6.0)
    queries = queries.reshape(COPIES, TOKENS, HEADS * HEAD_DIM)
    keyset = keyset.reshape(COPIES, TOKENS // QUERY_TILE, QUERY_TILE, HEADS * HEAD_DIM)
    return (queries, keyset)


def draw_query_rows(key, part):
    return drawn_draw(key)[0].astype(jnp.bfloat16)


def draw_key_rows(key, part):
    return drawn_draw(key)[1].astype(jnp.bfloat16)


def steps_of(rng, extent, cuts, smallest, high):
    loudness, own = 1.0, jax.random.fold_in(rng, 6)
    for dim, blocks in cuts:
        draws = jnp.exp(jax.random.uniform(jax.random.fold_in(own, dim), (blocks,), jnp.float32, smallest / len(cuts), high / len(cuts)))
        loudness = loudness * jnp.repeat(draws, extent[dim] // blocks).reshape([-1 if axis == dim else 1 for axis in range(len(extent))])
    return loudness


def bell_draw(key, dims, width, limit, shards=(), kind=jnp.bfloat16):
    result = width * jax.random.normal(key, dims, jnp.float32)
    if shards:
        result = result * steps_of(key, dims, shards, -0.22, 0.18)
    return jnp.clip(result, -limit, limit).astype(kind)


def setup_inputs(seed: int = 0) -> dict:
    streams_of = jax.random.split(jax.random.key(seed), 12)
    return {
        "pair_rep": bell_draw(streams_of[0], (TOKENS, N_QI, QUERY_TILE, PAIR), 1.0, 6.0, ((0, 2), (2, 2))),
        "query_rows": draw_query_rows(jax.random.fold_in(streams_of[11], 71), 0),
        "key_rows": draw_key_rows(jax.random.fold_in(streams_of[11], 71), 0),
        "value_rows": bell_draw(streams_of[3], (COPIES, N_QI, QUERY_TILE, WIDTH), 1.0, 6.0, ((0, 8), (2, 2))),
        "output_grad": bell_draw(streams_of[4], (COPIES, TOKENS, WIDTH), (TOKENS / 32), 24.0, ((0, 8), (1, 2))),
        "gain_first": jnp.clip(1.0 + 0.1 * jax.random.normal(streams_of[5], (PAIR,), jnp.float32), 0.5, 1.5),
        "gate_weight": bell_draw(streams_of[6], (PAIR, FF), PAIR ** -0.5, 0.5),
        "up_weight": bell_draw(streams_of[7], (PAIR, FF), PAIR ** -0.5, 0.5),
        "down_weight": bell_draw(streams_of[8], (FF, PAIR), FF ** -0.5, 0.25),
        "gain_second": jnp.clip(1.0 + 0.1 * jax.random.normal(streams_of[9], (PAIR,), jnp.float32), 0.5, 1.5),
        "head_weight": bell_draw(streams_of[10], (PAIR, HEADS), PAIR ** -0.5, 0.5),
    }


epsilon = 1e-05

def layer_norm(values, gain_vec):
    center = values - lax.optimization_barrier(jnp.mean(values, axis=1, keepdims=True))
    inverse = lax.rsqrt(lax.optimization_barrier(jnp.mean(center * center, axis=1, keepdims=True)) + epsilon)
    normed = center * inverse
    return (normed, inverse, normed * gain_vec)

def norm_backward(normed_grad, normed, inverse):
    first_mean = lax.optimization_barrier(jnp.mean(normed_grad, axis=1, keepdims=True))
    second_mean = lax.optimization_barrier(jnp.mean(normed_grad * normed, axis=1, keepdims=True))
    return inverse * (normed_grad - first_mean - normed * second_mean)

def wide_einsum(form, left, right):
    return jnp.einsum(form, left.astype(jnp.float32), right.astype(jnp.float32))

def transition_forward(cells, params):
    gain_first, gate_weight, up_weight, down_weight, gain_second, head_weight = params
    inputs = cells.astype(jnp.float32)
    pre_normed, pre_inverse, pre_scaled = layer_norm(inputs, gain_first)
    pre_lowered = pre_scaled.astype(jnp.bfloat16)
    gate_pre = jnp.dot(pre_lowered, gate_weight, preferred_element_type=jnp.float32)
    up_pre = jnp.dot(pre_lowered, up_weight, preferred_element_type=jnp.float32)
    gate_sigmoid = jax.nn.sigmoid(gate_pre)
    hidden = (gate_pre * gate_sigmoid * up_pre).astype(jnp.bfloat16)
    updated = inputs + jnp.dot(hidden, down_weight, preferred_element_type=jnp.float32)
    post_normed, post_inverse, post_scaled = layer_norm(updated, gain_second)
    post_lowered = post_scaled.astype(jnp.bfloat16)
    bias_heads = wide_einsum('mc,ch->hm', post_lowered, head_weight).astype(jnp.bfloat16)
    saved_state = (pre_normed, pre_inverse, pre_lowered, gate_pre, up_pre, gate_sigmoid, hidden, post_normed, post_inverse, post_lowered)
    return (bias_heads, saved_state)

def transition_backward(saved_state, grad_heads, params):
    gain_first, gate_weight, up_weight, down_weight, gain_second, head_weight = params
    pre_normed, pre_inverse, pre_lowered, gate_pre, up_pre, gate_sigmoid, hidden, post_normed, post_inverse, post_lowered = saved_state
    grad_low = grad_heads.astype(jnp.bfloat16)
    post_scaled = wide_einsum('hm,ch->mc', grad_low, head_weight)
    head_part = wide_einsum('mc,hm->ch', post_lowered, grad_low)
    second_part = lax.optimization_barrier(jnp.sum(post_scaled * post_normed, axis=0))
    updated_grad = norm_backward(post_scaled * gain_second, post_normed, post_inverse)
    updated_low = updated_grad.astype(jnp.bfloat16)
    down_part = wide_einsum('mf,mc->fc', hidden, updated_low)
    hidden_grad = wide_einsum('mc,fc->mf', updated_low, down_weight)
    gate_low = (hidden_grad * up_pre * gate_sigmoid * (1.0 + gate_pre * (1.0 - gate_sigmoid))).astype(jnp.bfloat16)
    up_low = (hidden_grad * gate_pre * gate_sigmoid).astype(jnp.bfloat16)
    gate_part = wide_einsum('mc,mf->cf', pre_lowered, gate_low)
    up_part = wide_einsum('mc,mf->cf', pre_lowered, up_low)
    pre_scaled = wide_einsum('mf,cf->mc', gate_low, gate_weight) + wide_einsum('mf,cf->mc', up_low, up_weight)
    first_part = lax.optimization_barrier(jnp.sum(pre_scaled * pre_normed, axis=0))
    inputs_grad = norm_backward(pre_scaled * gain_first, pre_normed, pre_inverse)
    pair_low = (updated_grad + inputs_grad).astype(jnp.bfloat16)
    return (pair_low, (gate_part, up_part, down_part, head_part, first_part, second_part))

def reference(pair_rep, query_rows, key_rows, value_rows, output_grad, gain_first, gate_weight, up_weight, down_weight, gain_second, head_weight):
    params = (gain_first, gate_weight, up_weight, down_weight, gain_second, head_weight)
    score_scale = HEAD_DIM ** (-0.5)
    block_count = TOKENS // ROWS_SUB
    pair_full = pair_rep.reshape(block_count, ROWS_SUB * TOKENS, PAIR)
    bias_blocks = lax.map(lambda cells: transition_forward(cells, params)[0], pair_full)
    bias_full = bias_blocks.reshape(block_count, HEADS, ROWS_SUB, TOKENS).transpose(1, 0, 2, 3).reshape(HEADS, TOKENS, TOKENS)
    keys_all = key_rows.reshape(COPIES, TOKENS, WIDTH)
    values_all = value_rows.reshape(COPIES, TOKENS, WIDTH)

    def one_copy(running, items):
        query_copy, key_copy, value_copy, grad_copy = items
        query_tile = query_copy.astype(jnp.float32).reshape(TOKENS, HEADS, HEAD_DIM)
        keys_tile = key_copy.astype(jnp.float32).reshape(TOKENS, HEADS, HEAD_DIM)
        values_tile = value_copy.astype(jnp.float32).reshape(TOKENS, HEADS, HEAD_DIM)
        grad_tile = grad_copy.astype(jnp.float32).reshape(TOKENS, HEADS, HEAD_DIM)
        scores = jnp.einsum('qhd,khd->hqk', query_tile, keys_tile) * score_scale + bias_full.astype(jnp.float32)
        largest = lax.optimization_barrier(jnp.max(scores, axis=2, keepdims=True))
        expo = jnp.exp(scores - largest)
        attend = expo / lax.optimization_barrier(jnp.sum(expo, axis=2, keepdims=True))
        attend_grad = jnp.einsum('qhd,khd->hqk', grad_tile, values_tile)
        delta = lax.optimization_barrier(jnp.sum(attend * attend_grad, axis=2, keepdims=True))
        score_grad = attend * (attend_grad - delta)
        score_low = score_grad.astype(jnp.bfloat16).astype(jnp.float32)
        attend_low = attend.astype(jnp.bfloat16).astype(jnp.float32)
        query_out = (jnp.einsum('hqk,khd->qhd', score_low, keys_tile) * score_scale).astype(jnp.bfloat16)
        key_out = (jnp.einsum('hqk,qhd->khd', score_low, query_tile) * score_scale).astype(jnp.bfloat16)
        value_out = jnp.einsum('hqk,qhd->khd', attend_low, grad_tile).astype(jnp.bfloat16)
        return (running + score_grad, (query_out.reshape(TOKENS, WIDTH), key_out.reshape(TOKENS, WIDTH), value_out.reshape(TOKENS, WIDTH)))
    initial = jnp.zeros((HEADS, TOKENS, TOKENS), jnp.float32)
    bias_sum, outputs = lax.scan(one_copy, initial, (query_rows, keys_all, values_all, output_grad))
    query_grad, key_grad, value_grad = outputs
    grad_blocks = bias_sum.reshape(HEADS, block_count, ROWS_SUB * TOKENS).transpose(1, 0, 2)

    def one_block(running, items):
        cells, grad_heads = items
        saved_state = transition_forward(cells, params)[1]
        pair_low, weight_parts = transition_backward(saved_state, grad_heads, params)
        return (tuple((total + part for total, part in zip(running, weight_parts))), pair_low)
    zeros_init = (jnp.zeros((PAIR, FF), jnp.float32), jnp.zeros((PAIR, FF), jnp.float32), jnp.zeros((FF, PAIR), jnp.float32), jnp.zeros((PAIR, HEADS), jnp.float32), jnp.zeros((PAIR,), jnp.float32), jnp.zeros((PAIR,), jnp.float32))
    reduced, pair_blocks = lax.scan(one_block, zeros_init, (pair_full, grad_blocks))
    pair_grad = pair_blocks.reshape(N_QI, COPIES, ROWS_SUB, N_QI, QUERY_TILE, PAIR)
    factor = 1.0 / TOKENS
    return (query_grad, key_grad, value_grad, pair_grad, reduced[0] * factor, reduced[1] * factor, reduced[2] * factor, reduced[3] * factor, reduced[4] * factor, reduced[5] * factor)
```

```python
import functools

import jax
import jax.numpy as jnp
from jax import lax
from jax.experimental import pallas as pl
from jax.experimental.pallas import tpu as pltpu
from jax.sharding import PartitionSpec as P

HEADS = 16
HEAD_DIM = 48
ALIGN = 16

epsilon = 1e-05
F32 = jnp.float32
BF16 = jnp.bfloat16
MESH = pl.DeviceIdType.MESH


def dot(left, right, left_dim, right_dim):
    return lax.dot_general(
        left, right, (((left_dim,), (right_dim,)), ((), ())), preferred_element_type=F32
    )


def normalize(values):
    center = values - jnp.mean(values, axis=1, keepdims=True)
    inverse = lax.rsqrt(jnp.mean(center * center, axis=1, keepdims=True) + epsilon)
    return center * inverse, inverse


def norm_backward(normed_grad, normed, inverse):
    first_mean = jnp.mean(normed_grad, axis=1, keepdims=True)
    second_mean = jnp.mean(normed_grad * normed, axis=1, keepdims=True)
    return inverse * (normed_grad - first_mean - normed * second_mean)


def kernel(
    sizes,
    pair_ref,
    q_ref,
    k_ref,
    v_ref,
    g_ref,
    gain_first_ref,
    gate_ref,
    up_ref,
    down_ref,
    gain_second_ref,
    head_ref,
    query_out,
    key_out,
    value_out,
    pair_out,
    weight_out,
    cells,
    pre_normed,
    pre_low,
    pre_low_t,
    gate_coef,
    up_coef,
    hidden,
    hidden_t,
    post_normed,
    post_low,
    inverses,
    bias_rows,
    bias_all,
    score,
    attend_grad,
    stats,
    grad_send,
    grad_recv,
    grad_sum,
    post_scaled,
    query_part,
    query_recv,
    kv_part,
    kv_recv,
    w_part,
    w_core,
    w_sum,
    w_recv,
    cell_sem,
    bias_send_sem,
    bias_recv_sem,
    stat_send_sem,
    stat_recv_sem,
    grad_send_sem,
    grad_recv_sem,
    query_send_sem,
    query_recv_sem,
    pair_sems,
    w_send_sem,
    w_recv_sem,
    all_send_sem,
    all_recv_sem,
    fwd_send_sem,
    fwd_recv_sem,
):
    n_noise, n_qi, n_kj, rows, keys, share, block = sizes
    group = n_noise * n_kj
    cell_count = share * keys
    chunk = min(256, cell_count)
    scale = HEAD_DIM ** (-0.5)
    noise = lax.axis_index("noise")
    qi = lax.axis_index("qi")
    kj = lax.axis_index("kj")
    me = noise * n_kj + kj
    sibling = {"qi": 1 - qi}
    channels = cells.shape[-1]
    width = q_ref.shape[-1]
    half = keys // n_qi
    q_half = rows // n_kj

    def remote(src, dst, send, recv, device):
        return pltpu.make_async_remote_copy(
            src_ref=src, dst_ref=dst, send_sem=send, recv_sem=recv, device_id=device, device_id_type=MESH
        )

    def of_group(index):
        return {"noise": index // n_kj, "kj": lax.rem(index, n_kj)}

    def each(count, body):
        def step(i, carry):
            body(i)
            return carry

        lax.fori_loop(1, count, step, 0)

    own = pltpu.make_async_copy(pair_ref.at[pl.ds(noise * share, share)], cells, cell_sem)
    own.start()

    barrier = pltpu.get_barrier_semaphore()

    def greet(i):
        pl.semaphore_signal(
            barrier, inc=1, device_id=of_group(lax.rem(me + i, group)), device_id_type=MESH
        )

    each(group, greet)
    pl.semaphore_signal(barrier, inc=1, device_id=sibling, device_id_type=MESH)
    own.wait()

    gain_first = gain_first_ref[...]
    gain_second = gain_second_ref[...]
    head_t = head_ref[...].astype(F32).T.astype(BF16)
    flat_cells = cells[...].reshape(cell_count, channels)
    for start in range(0, cell_count, chunk):
        at = slice(start, start + chunk)
        inputs = flat_cells[at].astype(F32)
        normed, inverse = normalize(inputs)
        lowered = (normed * gain_first).astype(BF16)
        gate_pre = dot(lowered, gate_ref[...], 1, 0)
        up_pre = dot(lowered, up_ref[...], 1, 0)
        sigmoid = jax.nn.sigmoid(gate_pre)
        silu = gate_pre * sigmoid
        low_hidden = (silu * up_pre).astype(BF16)
        updated = inputs + dot(low_hidden, down_ref[...], 1, 0)
        after, after_inverse = normalize(updated)
        after_low = (after * gain_second).astype(BF16)
        pre_normed[at] = normed
        pre_low[at] = lowered
        gate_coef[at] = up_pre * sigmoid * (1.0 + gate_pre * (1.0 - sigmoid))
        up_coef[at] = silu
        hidden[at] = low_hidden
        post_normed[at] = after
        post_low[at] = after_low
        inverses[at, 0:1] = inverse
        inverses[at, 1:2] = after_inverse
    for i in range(share):
        bias_rows[i] = dot(head_t, post_low[i * keys : (i + 1) * keys], 1, 1)
    for h in range(HEADS):
        bias_all[noise, h] = bias_rows[:, h, :].astype(BF16)

    pl.semaphore_wait(barrier, group)

    def bias_copy(slot, peer):
        return remote(
            bias_all.at[slot], bias_all.at[slot], bias_send_sem.at[peer], bias_recv_sem.at[slot], {"noise": peer}
        )

    each(n_noise, lambda i: bias_copy(noise, lax.rem(noise + i, n_noise)).start())

    def head_of(ref, h):
        return ref[:, h * HEAD_DIM : (h + 1) * HEAD_DIM]

    for h in range(HEADS):
        score[h] = dot(head_of(q_ref, h), head_of(k_ref, h), 1, 1) * scale
        attend_grad[h] = dot(head_of(g_ref, h), head_of(v_ref, h), 1, 1)

    def bias_wait(i):
        peer = lax.rem(noise + n_noise - i, n_noise)
        bias_copy(peer, peer).wait_recv()

    each(n_noise, bias_wait)

    for h in range(HEADS):
        full = score[h] + bias_all[:, h].astype(F32).reshape(rows, keys)
        largest = jnp.max(full, axis=1, keepdims=True)
        expo = jnp.exp(full - largest)
        score[h] = expo
        stats[kj, :, h : h + 1] = largest
        stats[kj, :, HEADS + h : HEADS + h + 1] = jnp.sum(expo, axis=1, keepdims=True)
        stats[kj, :, 2 * HEADS + h : 2 * HEADS + h + 1] = jnp.sum(
            expo * attend_grad[h], axis=1, keepdims=True
        )

    def stat_copy(slot, peer):
        return remote(
            stats.at[slot], stats.at[slot], stat_send_sem.at[peer], stat_recv_sem.at[slot], {"kj": peer}
        )

    each(n_kj, lambda i: stat_copy(kj, lax.rem(kj + i, n_kj)).start())
    hidden_t[...] = hidden[...].T
    pre_low_t[...] = pre_low[...].T

    def stat_wait(i):
        peer = lax.rem(kj + n_kj - i, n_kj)
        stat_copy(peer, peer).wait_recv()

    each(n_kj, stat_wait)

    parts = [stats[j] for j in range(n_kj)]
    row_max = parts[0][:, 0:HEADS]
    for part in parts[1:]:
        row_max = jnp.maximum(row_max, part[:, 0:HEADS])
    row_sum = jnp.zeros_like(row_max)
    row_dot = jnp.zeros_like(row_max)
    for part in parts:
        weight = jnp.exp(part[:, 0:HEADS] - row_max)
        row_sum += weight * part[:, HEADS : 2 * HEADS]
        row_dot += weight * part[:, 2 * HEADS : 3 * HEADS]
    factor = jnp.exp(stats[kj, :, 0:HEADS] - row_max) / row_sum
    delta = row_dot / row_sum
    for h in range(HEADS):
        attend = score[h] * factor[:, h : h + 1]
        score_grad = attend * (attend_grad[h] - delta[:, h : h + 1])
        score[h] = attend
        attend_grad[h] = score_grad
        grad_send[:, h] = score_grad.reshape(n_noise, share, keys).astype(BF16)

    def grad_copy(slot, peer):
        return remote(
            grad_send.at[peer], grad_recv.at[slot], grad_send_sem.at[peer], grad_recv_sem.at[slot], {"noise": peer}
        )

    each(n_noise, lambda i: grad_copy(noise, lax.rem(noise + i, n_noise)).start())

    for h in range(HEADS):
        at = slice(h * HEAD_DIM, (h + 1) * HEAD_DIM)
        value_at = slice(width + h * HEAD_DIM, width + (h + 1) * HEAD_DIM)
        score_low = attend_grad[h].astype(BF16)
        attend_low = score[h].astype(BF16)
        query_part[:, :, at] = (
            (dot(score_low, head_of(k_ref, h), 1, 0) * scale).astype(BF16).reshape(n_kj, q_half, HEAD_DIM)
        )
        kv_part[:, :, at] = (
            (dot(score_low, head_of(q_ref, h), 0, 0) * scale).astype(BF16).reshape(n_qi, half, HEAD_DIM)
        )
        kv_part[:, :, value_at] = (
            dot(attend_low, head_of(g_ref, h), 0, 0).astype(BF16).reshape(n_qi, half, HEAD_DIM)
        )

    def query_copy(slot, peer):
        return remote(
            query_part.at[peer], query_recv.at[slot], query_send_sem.at[peer], query_recv_sem.at[slot], {"kj": peer}
        )

    each(n_kj, lambda i: query_copy(kj, lax.rem(kj + i, n_kj)).start())
    kv_copy = remote(kv_part.at[1 - qi], kv_recv, pair_sems.at[0], pair_sems.at[1], sibling)
    kv_copy.start()

    def grad_wait(i):
        peer = lax.rem(noise + n_noise - i, n_noise)
        grad_copy(peer, peer).wait_recv()

    grad_sum[...] = grad_send[noise].astype(F32)

    def grad_add(i):
        grad_wait(i)
        peer = lax.rem(noise + n_noise - i, n_noise)
        grad_sum[...] += grad_recv[peer].astype(F32)

    each(n_noise, grad_add)

    head_part = jnp.zeros((HEADS, channels), F32)
    for i in range(share):
        at = slice(i * keys, (i + 1) * keys)
        grad_low = grad_sum[:, i, :].astype(BF16)
        post_scaled[at] = dot(grad_low, head_t, 0, 0)
        head_part += dot(grad_low, post_low[at], 1, 0)
    hidden_count = gate_ref.shape[1]
    tiles = hidden_count // channels
    first_part = jnp.zeros((1, channels), F32)
    second_part = jnp.zeros((1, channels), F32)
    down_part = jnp.zeros((hidden_count, channels), F32)
    gate_part = jnp.zeros((channels, hidden_count), F32)
    up_part = jnp.zeros((channels, hidden_count), F32)
    for start in range(0, cell_count, chunk):
        at = slice(start, start + chunk)
        scaled = post_scaled[at]
        after = post_normed[at]
        second_part += jnp.sum(scaled * after, axis=0, keepdims=True)
        updated_grad = norm_backward(scaled * gain_second, after, inverses[at, 1:2])
        updated_low = updated_grad.astype(BF16)
        down_part += dot(hidden_t[:, at], updated_low, 1, 0)
        hidden_grad = dot(updated_low, down_ref[...], 1, 1)
        gate_low = (hidden_grad * gate_coef[at]).astype(BF16)
        up_low = (hidden_grad * up_coef[at]).astype(BF16)
        gate_part += dot(pre_low_t[:, at], gate_low, 1, 0)
        up_part += dot(pre_low_t[:, at], up_low, 1, 0)
        pre_scaled = dot(gate_low, gate_ref[...], 1, 1) + dot(up_low, up_ref[...], 1, 1)
        normed = pre_normed[at]
        first_part += jnp.sum(pre_scaled * normed, axis=0, keepdims=True)
        inputs_grad = norm_backward(pre_scaled * gain_first, normed, inverses[at, 0:1])
        pair_out[at] = (updated_grad + inputs_grad).astype(BF16)

    for t in range(tiles):
        at = slice(t * channels, (t + 1) * channels)
        w_part[at] = gate_part[:, at].astype(BF16)
        w_part[hidden_count + t * channels : hidden_count + (t + 1) * channels] = up_part[:, at].astype(BF16)
    w_part[2 * hidden_count : 3 * hidden_count] = down_part.astype(BF16)
    tail = 3 * hidden_count
    w_part[tail : tail + HEADS] = head_part.astype(BF16)
    w_part[tail + HEADS : tail + 2 * HEADS] = jnp.concatenate(
        (
            jnp.broadcast_to(first_part, (HEADS // 2, channels)),
            jnp.broadcast_to(second_part, (HEADS // 2, channels)),
        ),
        0,
    ).astype(BF16)
    if w_part.shape[0] > tail + 2 * HEADS:
        w_part[tail + 2 * HEADS :] = jnp.zeros((w_part.shape[0] - tail - 2 * HEADS, channels), BF16)

    span = group * block

    def half_rows(index):
        return pl.ds(pl.multiple_of(index * span, ALIGN), span)

    core_copy = remote(w_part.at[half_rows(1 - qi)], w_core, pair_sems.at[2], pair_sems.at[3], sibling)
    core_copy.start()

    total = query_part[kj].astype(F32)

    def query_add(i, total):
        peer = lax.rem(kj + n_kj - i, n_kj)
        query_copy(peer, peer).wait_recv()
        return total + query_recv[peer].astype(F32)

    query_out[...] = lax.fori_loop(1, n_kj, query_add, total).astype(BF16)
    kv_copy.wait_recv()
    kv_total = kv_part[qi].astype(F32) + kv_recv[...].astype(F32)
    key_out[...] = kv_total[:, :width].astype(BF16)
    value_out[...] = kv_total[:, width:].astype(BF16)

    core_copy.wait_recv()
    w_sum[...] = (w_part[half_rows(qi)].astype(F32) + w_core[...].astype(F32)).astype(BF16)

    def own_rows(index):
        return pl.ds(pl.multiple_of(index * block, ALIGN), block)

    def w_copy(slot, peer):
        return remote(
            w_sum.at[own_rows(peer)], w_recv.at[slot], w_send_sem.at[peer], w_recv_sem.at[slot], of_group(peer)
        )

    each(group, lambda i: w_copy(me, lax.rem(me + i, group)).start())

    def w_add(i, total):
        peer = lax.rem(me + group - i, group)
        w_copy(peer, peer).wait_recv()
        return total + w_recv[peer].astype(F32)

    total = lax.fori_loop(1, group, w_add, w_sum[own_rows(me)].astype(F32))

    def out_rows(core, index):
        return pl.ds(pl.multiple_of((core * group + index) * block, ALIGN), block)

    mine = out_rows(qi, me)
    weight_out[mine] = (total * (1.0 / (rows * n_qi))).astype(BF16)

    def all_copy(slot, peer):
        at = out_rows(qi, slot)
        return remote(weight_out.at[at], weight_out.at[at], all_send_sem.at[peer], all_recv_sem.at[slot], of_group(peer))

    def fwd_copy(core, slot):
        at = out_rows(core, slot)
        return remote(weight_out.at[at], weight_out.at[at], fwd_send_sem.at[slot], fwd_recv_sem.at[slot], sibling)

    each(group, lambda i: all_copy(me, lax.rem(me + i, group)).start())
    fwd_copy(qi, me).start()

    def forward(i):
        peer = lax.rem(me + group - i, group)
        all_copy(peer, peer).wait_recv()
        fwd_copy(qi, peer).start()

    each(group, forward)

    def fwd_wait(i, carry):
        fwd_copy(1 - qi, i).wait_recv()
        fwd_copy(qi, i).wait_send()
        return carry

    lax.fori_loop(0, group, fwd_wait, 0)

    def drain(i):
        peer = lax.rem(me + i, group)
        w_copy(me, peer).wait_send()
        all_copy(me, peer).wait_send()

    each(group, drain)

    def drain_noise(i):
        peer = lax.rem(noise + i, n_noise)
        bias_copy(noise, peer).wait_send()
        grad_copy(noise, peer).wait_send()

    each(n_noise, drain_noise)

    def drain_kj(i):
        peer = lax.rem(kj + i, n_kj)
        stat_copy(kj, peer).wait_send()
        query_copy(kj, peer).wait_send()

    each(n_kj, drain_kj)
    kv_copy.wait_send()
    core_copy.wait_send()


def finish(hidden_count, weight_ref, gate_out, up_out, down_out, head_out, first_out, second_out):
    channels = weight_ref.shape[1]
    for t in range(hidden_count // channels):
        at = slice(t * channels, (t + 1) * channels)
        gate_out[:, at] = weight_ref[at].astype(F32)
        up_out[:, at] = weight_ref[hidden_count + t * channels : hidden_count + (t + 1) * channels].astype(F32)
    down_out[...] = weight_ref[2 * hidden_count : 3 * hidden_count].astype(F32)
    tail = 3 * hidden_count
    head_out[...] = weight_ref[tail : tail + HEADS].astype(F32).T
    small = weight_ref[tail + HEADS : tail + 2 * HEADS].astype(F32)
    first_out[...] = small[0:1]
    second_out[...] = small[HEADS // 2 : HEADS // 2 + 1]


def local(
    mesh_shape,
    pair_rep,
    query_rows,
    key_rows,
    value_rows,
    output_grad,
    gain_first,
    gate_weight,
    up_weight,
    down_weight,
    gain_second,
    head_weight,
):
    n_noise, n_qi, n_kj = mesh_shape
    rows, block_count, block_rows, channels = pair_rep.shape
    keys = block_count * block_rows
    width = query_rows.shape[2]
    share = rows // n_noise
    count = share * keys
    group = n_noise * n_kj
    hidden_count = gate_weight.shape[1]
    total_rows = 3 * hidden_count + 2 * HEADS
    block = -(-total_rows // (n_qi * group * ALIGN)) * ALIGN
    half = keys // n_qi
    q_half = rows // n_kj
    sizes = (n_noise, n_qi, n_kj, rows, keys, share, block)
    vmem = pl.BlockSpec(memory_space=pltpu.VMEM)
    dma = pltpu.SemaphoreType.DMA
    span = n_qi * group * block

    scratch = [
        pltpu.VMEM((share, block_count, block_rows, channels), BF16),
        pltpu.VMEM((count, channels), F32),
        pltpu.VMEM((count, channels), BF16),
        pltpu.VMEM((channels, count), BF16),
        pltpu.VMEM((count, hidden_count), F32),
        pltpu.VMEM((count, hidden_count), F32),
        pltpu.VMEM((count, hidden_count), BF16),
        pltpu.VMEM((hidden_count, count), BF16),
        pltpu.VMEM((count, channels), F32),
        pltpu.VMEM((count, channels), BF16),
        pltpu.VMEM((count, 128), F32),
        pltpu.VMEM((share, HEADS, keys), F32),
        pltpu.VMEM((n_noise, HEADS, share, keys), BF16),
        pltpu.VMEM((HEADS, rows, keys), F32),
        pltpu.VMEM((HEADS, rows, keys), F32),
        pltpu.VMEM((n_kj, rows, 128), F32),
        pltpu.VMEM((n_noise, HEADS, share, keys), BF16),
        pltpu.VMEM((n_noise, HEADS, share, keys), BF16),
        pltpu.VMEM((HEADS, share, keys), F32),
        pltpu.VMEM((count, channels), F32),
        pltpu.VMEM((n_kj, q_half, width), BF16),
        pltpu.VMEM((n_kj, q_half, width), BF16),
        pltpu.VMEM((n_qi, half, 2 * width), BF16),
        pltpu.VMEM((half, 2 * width), BF16),
        pltpu.VMEM((span, channels), BF16),
        pltpu.VMEM((group * block, channels), BF16),
        pltpu.VMEM((group * block, channels), BF16),
        pltpu.VMEM((group, block, channels), BF16),
        dma(()),
        dma((n_noise,)),
        dma((n_noise,)),
        dma((n_kj,)),
        dma((n_kj,)),
        dma((n_noise,)),
        dma((n_noise,)),
        dma((n_kj,)),
        dma((n_kj,)),
        dma((4,)),
        dma((group,)),
        dma((group,)),
        dma((group,)),
        dma((group,)),
        dma((group,)),
        dma((group,)),
    ]
    query_grad, key_grad, value_grad, pair_grad, weights = pl.pallas_call(
        functools.partial(kernel, sizes),
        out_shape=(
            jax.ShapeDtypeStruct((q_half, width), BF16),
            jax.ShapeDtypeStruct((half, width), BF16),
            jax.ShapeDtypeStruct((half, width), BF16),
            jax.ShapeDtypeStruct((count, channels), BF16),
            jax.ShapeDtypeStruct((span, channels), BF16),
        ),
        in_specs=[pl.BlockSpec(memory_space=pl.ANY)] + [vmem] * 10,
        out_specs=(vmem,) * 5,
        scratch_shapes=scratch,
        compiler_params=pltpu.CompilerParams(
            collective_id=0, has_side_effects=True, vmem_limit_bytes=60 * 1024 * 1024
        ),
        name="block_backward",
    )(
        pair_rep,
        query_rows.reshape(rows, width),
        key_rows.reshape(keys, width),
        value_rows.reshape(keys, width),
        output_grad.reshape(rows, width),
        gain_first.reshape(1, channels),
        gate_weight,
        up_weight,
        down_weight,
        gain_second.reshape(1, channels),
        head_weight,
    )
    gate_grad, up_grad, down_grad, head_grad, first_grad, second_grad = pl.pallas_call(
        functools.partial(finish, hidden_count),
        out_shape=(
            jax.ShapeDtypeStruct((channels, hidden_count), F32),
            jax.ShapeDtypeStruct((channels, hidden_count), F32),
            jax.ShapeDtypeStruct((hidden_count, channels), F32),
            jax.ShapeDtypeStruct((channels, HEADS), F32),
            jax.ShapeDtypeStruct((1, channels), F32),
            jax.ShapeDtypeStruct((1, channels), F32),
        ),
        in_specs=[vmem],
        out_specs=(vmem,) * 6,
        name="finish_weights",
    )(weights)
    return (
        query_grad[None],
        key_grad[None],
        value_grad[None],
        pair_grad.reshape(1, 1, share, block_count, block_rows, channels),
        gate_grad,
        up_grad,
        down_grad,
        head_grad,
        first_grad.reshape(channels),
        second_grad.reshape(channels),
    )


def solution(mesh):
    mesh_shape = (mesh.shape["noise"], mesh.shape["qi"], mesh.shape["kj"])
    return jax.shard_map(
        functools.partial(local, mesh_shape),
        mesh=mesh,
        in_specs=(
            P("qi", None, "kj", None),
            P("noise", "qi", None),
            P("noise", None, "kj", None),
            P("noise", None, "kj", None),
            P("noise", "qi", None),
            P(),
            P(),
            P(),
            P(),
            P(),
            P(),
        ),
        out_specs=(
            P("noise", ("qi", "kj"), None),
            P("noise", ("qi", "kj"), None),
            P("noise", ("qi", "kj"), None),
            P("qi", "noise", None, None, "kj", None),
            P(),
            P(),
            P(),
            P(),
            P(),
            P(),
        ),
        check_vma=False,
    )
```
